32 devices in a mesh: parts: 2 (over y), blk: 4 (over z), row: 2 (over x), sub: 2 (over core).
Axes of the slice: x: 2, y: 2, z: 4, core: 2. Of those that a mesh axis runs over, the one named last changes fastest.
Arguments:
- query_grads: bfloat16 [512, 4, 2048], P('blk', None, 'sub'), may hold values from -6 to 6
- curvature: bfloat16 [4, 2048, 2048], P('blk', ('row', 'sub')), may hold values from -0.125 to 0.125
- train_grads: bfloat16 [5120, 4, 2048], P(('parts', 'row', 'sub'), 'blk'), parts along dimension 0, may hold values from -0.0625 to 0.0625
- query_ids: int32 [1024], P('parts'), parts along dimension 0, may hold values from 0 to 511, each once
- block_map: int32 [4], replicated, may hold values from 0 to 3, each once
- row_ids: int32 [5120], P(('parts', 'row', 'sub')), parts along dimension 0, may hold values from 0 to 639
Outputs:
- scores: float32 [512, 5120], P('blk', ('parts', 'row', 'sub')), parts along dimension 1
The draws below stay inside these ranges and needn't reach their ends.
There are 2 independent parts, one for each index of `parts`. The reference program is written for one: setup_inputs(seed, part) draws one part's arguments, and reference() takes and returns one part's arrays. A program takes and returns all parts, laid end to end along the dimension named above; an argument that names none is the same for every part. Nothing has to cross between parts.
Inputs may be any that keep to these rules, and one draw needn't show every extreme that they name: `query_ids`: each value appears once. `block_map`: each value appears once.
All inputs are finite; a program needn't handle non-finite values.
Results may differ from the reference program's by a relative error of at most 0.0029.
Values may be sent and summed in bfloat16 or wider, within the bound.
No kernel may reach another device: no remote copies, remote signals or barrier semaphores. Data moves between devices by JAX's collectives and lax.ppermute only.
A program may use at most 64 MiB of HBM per device.

```python
import jax
import jax.numpy as jnp
from jax import lax

K = 2048
Q = 512
R_DEV = 640
L = 4
R = 2560


def with_ends(values, key, least, largest):
    longest = values.shape.index(max(values.shape))
    spots = []
    for shift in (0, 1):
        where = [jax.random.randint(jax.random.fold_in(key, axis), (), 0, length) for axis, length in enumerate(values.shape)]
        where[longest] = (where[longest] + shift) % values.shape[longest]
        spots.append(tuple(where))
    return values.at[spots[0]].set(least).at[spots[1]].set(largest)


def with_spikes(entries, rng, source, target, shards_of, factor):
    def block_of(position):
        return (jnp.arange(entries.shape[position]) // (entries.shape[position] // shards_of)).reshape((-1,) + (1,) * (entries.ndim - 1 - position))

    one_side = jax.random.permutation(rng, shards_of)[block_of(target)]
    far = (block_of(target) + shards_of // 2) % shards_of
    return jnp.where((block_of(source) == one_side) | (block_of(source) == far), factor * entries, entries)


def shard_levels(key, dims, shards, smallest, largest):
    def one(position, shards_of):
        steps = jax.random.uniform(jax.random.fold_in(jax.random.fold_in(key, 6), position), (shards_of,), jnp.float32, smallest / len(shards), largest / len(shards))
        return jnp.repeat(jnp.exp(steps), dims[position] // shards_of).reshape((-1,) + (1,) * (len(dims) - position - 1))

    gain = one(*shards[0])
    for cut in shards[1:]:
        gain = gain * one(*cut)
    return gain


def bell_draw(own_key, shape, width, bound, split=(), held_as=jnp.bfloat16):
    array = jax.random.normal(own_key, shape, jnp.float32) * width
    if len(split) > 0:
        array = shard_levels(own_key, shape, split, -0.22, 0.18) * array
    return jnp.clip(array, min=-bound, max=bound).astype(held_as)


def noise_with(own_key, dims, spread, most, shards, heavy, kind=jnp.bfloat16):
    drawn = spread * jax.random.normal(own_key, dims, jnp.float32)
    if shards:
        drawn = drawn * shard_levels(own_key, dims, shards, -0.22, 0.18)
    return jnp.clip(with_spikes(drawn, jax.random.fold_in(own_key, 3), *heavy), -most, most).astype(kind)


def setup_inputs(seed: int = 0, part: int = 0) -> dict:
    splits = jax.random.split(jax.random.key(seed), 7)
    part_keys = jax.random.split(jax.random.fold_in(splits[6], part), 7)
    return {
        "query_grads": noise_with(splits[0], (Q, L, K), 1.0, 6.0, ((0, 4), (2, 2)), (1, 0, 4, 2.0)),
        "curvature": bell_draw(splits[1], (L, K, K), K ** -0.5, 0.125, ((0, 4), (1, 4))),
        "train_grads": bell_draw(part_keys[2], (R, L, K), (L * K) ** -0.5, 0.0625, ((0, 4), (1, 4))),
        "query_ids": jax.random.permutation(part_keys[3], Q).astype(jnp.int32),
        "block_map": jax.random.permutation(splits[4], L).astype(jnp.int32),
        "row_ids": with_ends(jax.random.randint(part_keys[5], (R,), 0, R_DEV), jax.random.fold_in(part_keys[5], 1), 0, R_DEV - 1).astype(jnp.int32),
    }


def reference(query_grads, curvature, train_grads, query_ids, block_map, row_ids):
    grouped = jnp.take(query_grads, block_map, axis=1)

    def one_slot(pair):
        block, grads = pair
        return jnp.dot(grads, block.T, preferred_element_type=jnp.float32).astype(jnp.bfloat16)

    precond = lax.map(one_slot, (curvature, jnp.swapaxes(grouped, 0, 1)))
    precond = jnp.swapaxes(precond, 0, 1)
    total_rows = row_ids.shape[0]
    starts = (jnp.arange(total_rows, dtype=jnp.int32) // R_DEV) * R_DEV
    chosen = jnp.take(train_grads, (starts + row_ids).astype(jnp.int32), axis=0)
    flat_q = precond.reshape(precond.shape[0], -1)
    flat_r = chosen.reshape(chosen.shape[0], -1)
    total = jnp.dot(flat_q, flat_r.T, preferred_element_type=jnp.float32)
    scores = jnp.zeros(total.shape, jnp.float32).at[query_ids].set(total)
    return scores
```

```python
import functools

import jax
import jax.numpy as jnp
from jax import lax
from jax.sharding import PartitionSpec as P


def swaps(n):
    if n & (n - 1) == 0:
        return [(lambda i, d=d: i ^ d) for d in range(n)], [(lambda i, d=d: i ^ d) for d in range(n)]
    return [(lambda i, d=d: (i + d) % n) for d in range(n)], [(lambda i, d=d: (i - d) % n) for d in range(n)]


def per_device(sizes, query_grads, curvature, train_grads, query_ids, block_map, row_ids):
    n_parts, n_blk, n_row, n_sub = (sizes[a] for a in ("parts", "blk", "row", "sub"))
    part, blk, row, sub = (lax.axis_index(a) for a in ("parts", "blk", "row", "sub"))
    to_part, from_part = swaps(n_parts)
    to_blk, from_blk = swaps(n_blk)
    to_row, from_row = swaps(n_row)
    to_sub, from_sub = swaps(n_sub)
    owned, half = query_grads.shape[0], query_grads.shape[2]
    mine_q = owned // n_parts
    n_feat = curvature.shape[1]
    queries = owned * n_blk

    def send(x, axes, pairs):
        return lax.ppermute(x, axes, pairs)

    blk_pairs = [[(i, to_blk[d](i)) for i in range(n_blk)] for d in range(n_blk)]
    sub_pairs = [[(i, to_sub[d](i)) for i in range(n_sub)] for d in range(n_sub)]

    def plane_pairs(dp, dr):
        return [
            (a * n_row + b, to_part[dp](a) * n_row + to_row[dr](b)) for a in range(n_parts) for b in range(n_row)
        ]

    by_block = jnp.swapaxes(lax.dynamic_slice_in_dim(query_grads, part * mine_q, mine_q, 0), 0, 1)
    arrived = []
    for d in range(n_blk):
        piece = lax.dynamic_index_in_dim(by_block, block_map[to_blk[d](blk)], 0, keepdims=False)
        arrived.append(send(piece, "blk", blk_pairs[d]) if d else piece)
    arrived = jnp.concatenate(arrived, 0)

    block = curvature[0]
    total = 0
    for d in range(n_sub):
        have = send(arrived, "sub", sub_pairs[d]) if d else arrived
        columns = lax.dynamic_slice_in_dim(block, from_sub[d](sub) * half, half, 1)
        total = total + jnp.einsum("qj,ij->qi", have, columns, preferred_element_type=jnp.float32)
    precond = total.astype(jnp.bfloat16)

    chosen = jnp.take(train_grads[:, 0], row_ids, axis=0, mode="clip")
    partial_rows, ids = [], []
    got = {}
    for dp in range(n_parts):
        for dr in range(n_row):
            got[dp, dr] = send(precond, ("parts", "row"), plane_pairs(dp, dr)) if dp or dr else precond
    flat = jnp.concatenate([got[dp, dr] for dp in range(n_parts) for dr in range(n_row)], 1)
    flats = [send(flat, "sub", sub_pairs[ds]) if ds else flat for ds in range(n_sub)]
    for dp in range(n_parts):
        scores = 0
        for ds in range(n_sub):
            for dr in range(n_row):
                there = (from_row[dr](row) * n_sub + from_sub[ds](sub)) * n_feat
                at = (dp * n_row + dr) * n_feat
                scores = scores + jnp.einsum(
                    "qk,rk->qr",
                    flats[ds][:, at : at + n_feat],
                    lax.dynamic_slice_in_dim(chosen, there, n_feat, 1),
                    preferred_element_type=jnp.float32,
                )
        partial_rows.append(scores.astype(jnp.bfloat16))
        for d in range(n_blk):
            start = from_blk[d](blk) * owned + from_part[dp](part) * mine_q
            ids.append(lax.dynamic_slice_in_dim(query_ids, start, mine_q, 0))
    partial_rows = jnp.concatenate(partial_rows, 0)
    ids = jnp.concatenate(ids, 0)

    out = 0
    for d in range(n_blk):
        rows = to_blk[d](blk) * owned + lax.broadcasted_iota(jnp.int32, (owned, queries), 0)
        pick = (rows == ids[None, :]).astype(jnp.bfloat16)
        placed = jnp.einsum("oq,qr->or", pick, partial_rows, preferred_element_type=jnp.float32)
        if d:
            placed = send(placed.astype(jnp.bfloat16), "blk", blk_pairs[d]).astype(jnp.float32)
        out = out + placed
    return out


def solution(mesh):
    placed = (
        P("blk", None, "sub"),
        P("blk", ("row", "sub"), None),
        P(("parts", "row", "sub"), "blk", None),
        P("parts"),
        P(),
        P(("parts", "row", "sub")),
    )
    return jax.shard_map(
        functools.partial(per_device, dict(mesh.shape)),
        mesh=mesh,
        in_specs=placed,
        out_specs=P("blk", ("parts", "row", "sub")),
        check_vma=False,
    )
```
